32 devices in a mesh: dp: 8 (over z, y), mp: 4 (over x, core).
Axes of the slice: x: 2, y: 2, z: 4, core: 2. Of those that a mesh axis runs over, the one named last changes fastest.
Arguments:
- tokens: bfloat16 [9456, 1024], P('dp'), may hold values from -8 to 8
- masked_patches: int32 [48, 98], P('dp'), may hold values from 0 to 196, as said below
- mask_token: bfloat16 [1024], replicated, may hold values from -6 to 6
- norm1_gain: bfloat16 [1024], replicated, may hold values from 0.099609375 to 1.8984375
- norm1_bias: bfloat16 [1024], replicated, may hold values from -1.75 to 1.75
- query_weight: bfloat16 [1024, 1024], P(None, 'mp'), may hold values from -0.1875 to 0.1875
- query_bias: bfloat16 [1024], P('mp'), may hold values from -1.75 to 1.75
- key_weight: bfloat16 [1024, 1024], P(None, 'mp'), may hold values from -0.1875 to 0.1875
- value_weight: bfloat16 [1024, 1024], P(None, 'mp'), may hold values from -0.1875 to 0.1875
- value_bias: bfloat16 [1024], P('mp'), may hold values from -1.75 to 1.75
- out_weight: bfloat16 [1024, 1024], P('mp'), may hold values from -1.5 to 1.5
- out_bias: bfloat16 [1024], replicated, may hold values from -1.75 to 1.75
- attn_scale: bfloat16 [1024], replicated, may hold values from 0.5 to 1.5
- norm2_gain: bfloat16 [1024], replicated, may hold values from 0.099609375 to 1.8984375
- norm2_bias: bfloat16 [1024], replicated, may hold values from -1.75 to 1.75
- up_weight: bfloat16 [1024, 4096], P(None, 'mp'), may hold values from -0.1875 to 0.1875
- up_bias: bfloat16 [4096], P('mp'), may hold values from -1.75 to 1.75
- down_weight: bfloat16 [4096, 1024], P('mp'), may hold values from -0.1875 to 0.1875
- down_bias: bfloat16 [1024], replicated, may hold values from -1.75 to 1.75
- mlp_scale: bfloat16 [1024], replicated, may hold values from 0.5 to 1.5
- out_cotangent: bfloat16 [9456, 1024], P('dp'), may hold values from -6 to 6
Outputs:
- block_out: bfloat16 [9456, 1024], P('dp')
- tokens_grad: bfloat16 [9456, 1024], P('dp')
- grad_mask_token: float32 [1024], P('dp')
- grad_norm1_gain: float32 [1024], P('dp')
- grad_norm1_bias: float32 [1024], P('dp')
- grad_query_weight: float32 [1024, 1024], P('dp', 'mp')
- grad_query_bias: float32 [1024], P(('mp', 'dp'))
- grad_key_weight: float32 [1024, 1024], P('dp', 'mp')
- grad_value_weight: float32 [1024, 1024], P('dp', 'mp')
- grad_value_bias: float32 [1024], P(('mp', 'dp'))
- grad_out_weight: float32 [1024, 1024], P(('mp', 'dp'))
- grad_out_bias: float32 [1024], P('dp')
- grad_attn_scale: float32 [1024], P('dp')
- grad_norm2_gain: float32 [1024], P('dp')
- grad_norm2_bias: float32 [1024], P('dp')
- grad_up_weight: float32 [1024, 4096], P('dp', 'mp')
- grad_up_bias: float32 [4096], P(('mp', 'dp'))
- grad_down_weight: float32 [4096, 1024], P(('mp', 'dp'))
- grad_down_bias: float32 [1024], P('dp')
- grad_mlp_scale: float32 [1024], P('dp')
The draws below stay inside these ranges and needn't reach their ends.
Inputs may be any that keep to these rules, and one draw needn't show every extreme that they name: `masked_patches`: each row lists distinct patch positions first, 19 to 98 of them, the rest of the row being 0 (an empty slot); some image has 98 masked patches.
All inputs are finite; a program needn't handle non-finite values.
Results may differ from the reference program's by a relative error of at most 0.024.
Values sent between devices are 32-bit elements; how exact they have to be, the bound alone decides.
No kernel may reach another device: no remote copies, remote signals or barrier semaphores. Data moves between devices by JAX's collectives and lax.ppermute only.
A program may use at most 192 MiB of HBM per device.

```python
import jax
import jax.numpy as jnp
from jax import lax

D = 1024
H = 16
HD = 64
FF = 4096
PATCHES = 196
SEQ = 197
MAXM = 98
MINM = 19
IMAGES = 48
TOKENS = 9456


def draw_masked_patches(key, part):
    key_count = jax.random.fold_in(key, 11)
    key_order = jax.random.fold_in(key, 23)
    counts = jax.random.randint(key_count, (IMAGES,), MINM, MAXM + 1)
    counts = counts.at[0].set(MAXM)
    order_keys = jax.random.split(key_order, IMAGES)
    orders = jax.vmap(lambda one_key: jax.random.permutation(one_key, PATCHES))(order_keys) + 1
    lists = orders[:, :MAXM].astype(jnp.int32)
    first_row = lists[0]
    first_row = jnp.where(first_row == PATCHES, first_row[0], first_row).at[0].set(PATCHES)
    lists = lists.at[0].set(first_row)
    slots = jnp.arange(MAXM, dtype=jnp.int32)
    lists = jnp.where(slots[None, :] < counts[:, None], lists, 0)
    return lists.astype(jnp.int32)


def spiked(values, own_key, source, target, shards_of, factor):
    owner, partner = [(jnp.arange(values.shape[position]) // (values.shape[position] // shards_of)).reshape([-1 if axis == position else 1 for axis in range(values.ndim)]) for position in (source, target)]
    chosen = jax.random.permutation(own_key, shards_of)[partner]
    strong = (owner == chosen) | (owner == (partner + shards_of // 2) % shards_of)
    return jnp.where(strong, factor * values, values)


def block_levels(own_key, shape, cuts, low, largest):
    gain = 1.0
    for position, parts in cuts:
        draws = jax.random.uniform(jax.random.fold_in(jax.random.fold_in(own_key, 6), position), (parts,), jnp.float32, low / len(cuts), largest / len(cuts))
        gain = gain * jnp.repeat(jnp.exp(draws), shape[position] // parts).reshape((-1,) + (1,) * (len(shape) - 1 - position))
    return gain


def normal_values(key, shape, scale, most, cuts=(), held_as=jnp.bfloat16):
    array = scale * jax.random.normal(key, shape, jnp.float32)
    if cuts:
        array = array * block_levels(key, shape, cuts, -0.22, 0.18)
    return jnp.clip(array, -most, most).astype(held_as)


def bell_draw_with(own_key, dims, spread, most, cuts, heavy, kind=jnp.bfloat16):
    array = spread * jax.random.normal(own_key, dims, jnp.float32)
    if cuts:
        array = array * block_levels(own_key, dims, cuts, -0.22, 0.18)
    return jnp.clip(spiked(array, jax.random.fold_in(own_key, 3), *heavy), -most, most).astype(kind)


def setup_inputs(seed: int = 0) -> dict:
    splits = jax.random.split(jax.random.key(seed), 22)
    tokens = bell_draw_with(splits[0], (TOKENS, D), 1.0, 8.0, ((0, 8),), (0, 1, 8, 2.0))
    masked_patches = draw_masked_patches(jax.random.fold_in(splits[21], 71), 0)
    mask_token = normal_values(splits[2], (D,), 1.0, 6.0)
    norm1_gain = jnp.clip(1.0 + 0.18 * jax.random.normal(splits[3], (D,), jnp.float32), 0.099609375, 1.8984375).astype(jnp.bfloat16)
    norm1_bias = normal_values(splits[4], (D,), 0.3, 1.75)
    query_weight = normal_values(splits[5], (D, D), D ** -0.5, 0.1875, ((1, 4),))
    query_bias = normal_values(splits[6], (D,), 0.3, 1.75, ((0, 4),))
    key_weight = normal_values(splits[7], (D, D), D ** -0.5, 0.1875, ((1, 4),))
    value_weight = normal_values(splits[8], (D, D), D ** -0.5, 0.1875, ((1, 4),))
    value_bias = normal_values(splits[9], (D,), 0.3, 1.75, ((0, 4),))
    out_weight = normal_values(splits[10], (D, D), (D // 64) ** -0.5, 1.5, ((0, 4),))
    out_bias = normal_values(splits[11], (D,), 0.3, 1.75)
    attn_scale = jnp.clip(jax.random.uniform(splits[12], (D,), jnp.float32, 0.5, 1.5), 0.5, 1.5).astype(jnp.bfloat16)
    norm2_gain = jnp.clip(1.0 + 0.18 * jax.random.normal(splits[13], (D,), jnp.float32), 0.099609375, 1.8984375).astype(jnp.bfloat16)
    norm2_bias = normal_values(splits[14], (D,), 0.3, 1.75)
    up_weight = normal_values(splits[15], (D, FF), D ** -0.5, 0.1875, ((1, 4),))
    up_bias = normal_values(splits[16], (FF,), 0.3, 1.75, ((0, 4),))
    down_weight = normal_values(splits[17], (FF, D), (FF // 4) ** -0.5, 0.1875, ((0, 4),))
    down_bias = normal_values(splits[18], (D,), 0.3, 1.75)
    mlp_scale = jnp.clip(jax.random.uniform(splits[19], (D,), jnp.float32, 0.5, 1.5), 0.5, 1.5).astype(jnp.bfloat16)
    out_cotangent = normal_values(splits[20], (TOKENS, D), 1.0, 6.0, ((0, 8),))
    return {"tokens": tokens, "masked_patches": masked_patches, "mask_token": mask_token, "norm1_gain": norm1_gain, "norm1_bias": norm1_bias, "query_weight": query_weight, "query_bias": query_bias, "key_weight": key_weight, "value_weight": value_weight, "value_bias": value_bias, "out_weight": out_weight, "out_bias": out_bias, "attn_scale": attn_scale, "norm2_gain": norm2_gain, "norm2_bias": norm2_bias, "up_weight": up_weight, "up_bias": up_bias, "down_weight": down_weight, "down_bias": down_bias, "mlp_scale": mlp_scale, "out_cotangent": out_cotangent}


@jax.custom_vjp
def low(v):
    return lax.optimization_barrier(v.astype(jnp.bfloat16)).astype(jnp.float32)

@jax.custom_vjp
def low_back(v):
    return v

def low_keep(v):
    return (low(v), None)

def low_pass(kept, grad):
    return (grad,)

def back_keep(v):
    return (v, None)

def back_low(kept, grad):
    return (low(grad),)
low.defvjp(low_keep, low_pass)
low_back.defvjp(back_keep, back_low)
images_per_group = 16
norm_eps = 1e-06

def dot_high(left, right):
    return jnp.dot(left, right, precision=lax.Precision.HIGHEST, preferred_element_type=jnp.float32)

def layer_norm(values):
    mean_val = lax.optimization_barrier(jnp.mean(values, axis=-1, keepdims=True))
    centered = values - mean_val
    return centered * lax.rsqrt(lax.optimization_barrier(jnp.mean(centered * centered, axis=-1, keepdims=True)) + norm_eps)

def block(params, rows, mask_col):
    mask_row, gain_one, bias_one, w_query, b_query, w_key, w_value, b_value, w_out, b_out, scale_one, gain_two, bias_two, w_up, b_up, w_down, b_down, scale_two = params
    start = rows * (1.0 - mask_col) + mask_col * mask_row[None, :]
    attn_in = low(layer_norm(start) * gain_one + bias_one)
    queries = low(low_back(dot_high(attn_in, w_query) + b_query))
    key_rows = low(low_back(dot_high(attn_in, w_key)))
    value_rows = low(low_back(dot_high(attn_in, w_value) + b_value))
    count = rows.shape[0] // SEQ
    query_heads = queries.reshape(count, SEQ, H, HD)
    key_heads = key_rows.reshape(count, SEQ, H, HD)
    value_heads = value_rows.reshape(count, SEQ, H, HD)
    scores = jnp.einsum('gqhd,gkhd->ghqk', query_heads, key_heads, precision=lax.Precision.HIGHEST) * (1.0 / jnp.sqrt(jnp.float32(HD)))
    scores = low_back(scores)
    probs = jax.nn.softmax(scores, axis=-1)
    attended = jnp.einsum('ghqk,gkhd->gqhd', low(probs), value_heads, precision=lax.Precision.HIGHEST)
    attended = low(low_back(attended.reshape(rows.shape[0], D)))
    attn_branch = low_back(dot_high(attended, w_out)) + b_out
    middle = start + scale_one * attn_branch
    mlp_in = low(layer_norm(middle) * gain_two + bias_two)
    hidden = low_back(dot_high(mlp_in, w_up) + b_up)
    activated = low(jax.nn.gelu(hidden, approximate=False))
    mlp_branch = low_back(dot_high(activated, w_down)) + b_down
    return middle + scale_two * mlp_branch

def reference(tokens, masked_patches, mask_token, norm1_gain, norm1_bias, query_weight, query_bias, key_weight, value_weight, value_bias, out_weight, out_bias, attn_scale, norm2_gain, norm2_bias, up_weight, up_bias, down_weight, down_bias, mlp_scale, out_cotangent):
    params = tuple((arr.astype(jnp.float32) for arr in (mask_token, norm1_gain, norm1_bias, query_weight, query_bias, key_weight, value_weight, value_bias, out_weight, out_bias, attn_scale, norm2_gain, norm2_bias, up_weight, up_bias, down_weight, down_bias, mlp_scale)))
    positions = jnp.arange(SEQ, dtype=jnp.int32)
    hits = (masked_patches[:, None, :] == positions[None, :, None]) & (positions[None, :, None] >= 1)
    masked = jnp.any(hits, axis=-1).astype(jnp.float32)
    groups = IMAGES // images_per_group
    group_rows = images_per_group * SEQ
    row_groups = tokens.astype(jnp.float32).reshape(groups, group_rows, D)
    mask_groups = masked.reshape(groups, group_rows, 1)
    cot_groups = out_cotangent.astype(jnp.float32).reshape(groups, group_rows, D)

    def step(totals, item):
        rows, mask_col, cot = item
        result, pullback = jax.vjp(lambda prm, rws: block(prm, rws, mask_col), params, rows)
        grad_params, grad_rows = pullback(cot)
        totals = jax.tree.map(lambda acc, new: acc + new, totals, grad_params)
        return (totals, (result, grad_rows))
    zeros = jax.tree.map(jnp.zeros_like, params)
    totals, (results, row_grads) = lax.scan(step, zeros, (row_groups, mask_groups, cot_groups))
    block_out = results.reshape(TOKENS, D).astype(jnp.bfloat16)
    tokens_grad = row_grads.reshape(TOKENS, D).astype(jnp.bfloat16)
    return (block_out, tokens_grad) + tuple(totals)
```

```python
import functools
import math

import jax
import jax.numpy as jnp
from jax import lax
from jax.experimental import pallas as pl
from jax.experimental.pallas import tpu as pltpu
from jax.sharding import PartitionSpec as P

HD = 64
CHUNKS = 2
NORM_EPS = 1e-06
ROOT_HALF = 0.7071067811865476
INV_ROOT_TAU = 0.3989422804014327
VMEM_LIMIT = 60 << 20

f32 = jnp.float32
bf16 = jnp.bfloat16


def dot(left, right):
    return lax.dot_general(left, right, (((1,), (0,)), ((), ())), preferred_element_type=f32)


def dot_lt(left, right):
    return lax.dot_general(left, right, (((0,), (0,)), ((), ())), preferred_element_type=f32)


def dot_rt(left, right):
    return lax.dot_general(left, right, (((1,), (1,)), ((), ())), preferred_element_type=f32)


def normalize(values):
    centered = values - jnp.mean(values, axis=-1, keepdims=True)
    inv_std = lax.rsqrt(jnp.mean(centered * centered, axis=-1, keepdims=True) + NORM_EPS)
    return centered * inv_std, inv_std


def norm_back(grad, gain, normed, inv_std):
    scaled = grad * gain
    return inv_std * (
        scaled
        - jnp.mean(scaled, axis=-1, keepdims=True)
        - normed * jnp.mean(scaled * normed, axis=-1, keepdims=True)
    )


def col_sum(values):
    return jnp.sum(values, axis=0, keepdims=True)


def start_of(tok, mask, token_row):
    return tok.astype(f32) * (1.0 - mask) + mask * token_row[...].astype(f32)


def head_probs(queries, keys, seq_len):
    scores = dot_rt(queries, keys) * (1.0 / math.sqrt(HD))
    valid = lax.broadcasted_iota(jnp.int32, scores.shape, 1) < seq_len
    scores = jnp.where(valid, scores, -1e30)
    top = jnp.max(scores, axis=-1, keepdims=True)
    weights = jnp.exp(scores - top)
    return weights * (1.0 / jnp.sum(weights, axis=-1, keepdims=True))


def attend_kernel(
    seq_len, tok, patches, token_row, gain, bias, wq, bq, wk, wv, bv,
    mask_o, attn_in_o, q_o, k_o, v_o, att_o,
):
    rows = tok.shape[1]
    slots = patches.shape[2]
    place = lax.broadcasted_iota(jnp.int32, (rows, slots), 0)
    named = (jnp.broadcast_to(patches[0], (rows, slots)) == place) & (place >= 1)
    mask = jnp.max(jnp.where(named, 1.0, 0.0), axis=-1, keepdims=True)
    mask_o[0] = mask
    normed, _ = normalize(start_of(tok[0], mask, token_row))
    attn_in = (normed * gain[...].astype(f32) + bias[...].astype(f32)).astype(bf16)
    attn_in_o[0] = attn_in
    q_o[0] = (dot(attn_in, wq[...]) + bq[...].astype(f32)).astype(bf16)
    k_o[0] = dot(attn_in, wk[...]).astype(bf16)
    v_o[0] = (dot(attn_in, wv[...]) + bv[...].astype(f32)).astype(bf16)
    for head in range(wq.shape[1] // HD):
        at = slice(head * HD, (head + 1) * HD)
        probs = head_probs(q_o[0, :, at], k_o[0, :, at], seq_len)
        att_o[0, :, at] = dot(probs.astype(bf16), v_o[0, :, at]).astype(bf16).astype(f32)


def widen_kernel(w, o):
    o[...] = w[...].astype(f32)


def mlp_kernel(
    pos, a0, a1, a2, a3, w0, w1, w2, w3, ob, s1, g2, b2, tok, mask, token_row, cot, s2, up, ub, down,
    ab_o, mlp_in_o, act_o, hg_o, send_o, keep_o, ubg_o, dbg_o, att_s, w_s, og_s,
):
    step = pl.program_id(0)
    rows = mlp_in_o.shape[0]
    width = a0.shape[1]
    half = keep_o.shape[1]

    @pl.when(step == 0)
    def _():
        for k, (a, w) in enumerate(((a0, w0), (a1, w1), (a2, w2), (a3, w3))):
            at = pl.ds(pl.multiple_of(pos[k] * width, width), width)
            att_s[:, at] = a[...].astype(bf16)
            w_s[at, :] = w[...].astype(bf16)
        ab_o[...] = dot(att_s[...], w_s[...]) + ob[...].astype(f32)
        send_o[...] = jnp.zeros_like(send_o)
        keep_o[...] = jnp.zeros_like(keep_o)
        dbg_o[...] = jnp.zeros_like(dbg_o)
        block = 40

        def one(i, carry):
            at = pl.ds(pl.multiple_of(i * block, block), block)
            mid = start_of(tok[at, :], mask[at, :], token_row) + s1[...].astype(f32) * ab_o[at, :]
            normed, _ = normalize(mid)
            mlp_in_o[at, :] = (normed * g2[...].astype(f32) + b2[...].astype(f32)).astype(bf16)
            scaled = cot[at, :].astype(f32) * s2[...].astype(f32)
            og_s[at, :] = scaled.astype(bf16)
            dbg_o[...] += col_sum(scaled)
            return carry

        lax.fori_loop(0, rows // block, one, 0)

    hidden = dot(mlp_in_o[...], up[...]) + ub[...].astype(f32)
    cdf = 0.5 * (1.0 + lax.erf(hidden * ROOT_HALF))
    pdf = jnp.exp(-0.5 * hidden * hidden) * INV_ROOT_TAU
    act_o[...] = (hidden * cdf).astype(bf16)
    act_grad = dot_rt(og_s[...], down[...])
    hg = (act_grad * (cdf + hidden * pdf)).astype(bf16)
    hg_o[...] = hg
    ubg_o[...] = col_sum(hg.astype(f32))
    mine = pl.ds(pl.multiple_of(pos[4] * half, half), half)
    other = pl.ds(pl.multiple_of(pos[5] * half, half), half)
    send_o[...] += dot_rt(hg, up[other, :])
    keep_o[...] += dot_rt(hg, up[mine, :])


def down_kernel(pos, act, down, cot, db, send_o, keep_o, scale_o):
    half = keep_o.shape[1]
    mine = pl.ds(pl.multiple_of(pos[4] * half, half), half)
    other = pl.ds(pl.multiple_of(pos[5] * half, half), half)
    send_o[...] = dot(act[...], down[:, other])
    keep_o[...] = dot(act[...], down[:, mine])
    scale_o[:, other] = col_sum(
        cot[:, other].astype(f32) * (send_o[...] + 0.25 * db[:, other].astype(f32))
    )
    scale_o[:, mine] = col_sum(
        cot[:, mine].astype(f32) * (keep_o[...] + 0.25 * db[:, mine].astype(f32))
    )


def back_kernel(
    seq_len, pos, gm, go, tok, mask, ab, cot, q, k, v, token_row, s1, g1, g2, wo, wq, wk, wv,
    mid_grad_o, attn_grad_o, qkv_o, send_o, keep_o, vec_o, full_s, ag_s,
):
    step = pl.program_id(0)
    half = gm.shape[2]
    width = q.shape[2]
    mine = pl.ds(pl.multiple_of(pos[4] * half, half), half)
    other = pl.ds(pl.multiple_of(pos[5] * half, half), half)

    @pl.when(step == 0)
    def _():
        vec_o[...] = jnp.zeros_like(vec_o)

    full_s[:, mine] = gm[0]
    full_s[:, other] = go[0]
    m = mask[0]
    start = start_of(tok[0], m, token_row)
    scale = s1[...].astype(f32)
    branch = ab[0]
    normed, inv_std = normalize(start + scale * branch)
    grad = full_s[...]
    vec_o[0:1, :] += 0.25 * col_sum(grad * normed)
    vec_o[1:2, :] += 0.25 * col_sum(grad)
    mid_grad = cot[0].astype(f32) + norm_back(grad, g2[...].astype(f32), normed, inv_std)
    mid_grad_o[0] = mid_grad
    vec_o[2:3, :] += 0.25 * col_sum(mid_grad * branch)
    scaled = mid_grad * scale
    vec_o[3:4, :] += 0.25 * col_sum(scaled)
    attn_grad_o[0] = scaled.astype(bf16)
    ag_s[...] = dot_rt(attn_grad_o[0], wo[...]).astype(bf16)
    root = 1.0 / math.sqrt(HD)
    for head in range(width // HD):
        at = slice(head * HD, (head + 1) * HD)
        qh, kh, vh, ah = q[0, :, at], k[0, :, at], v[0, :, at], ag_s[:, at]
        probs = head_probs(qh, kh, seq_len)
        prob_grad = dot_rt(ah, vh)
        inner = jnp.sum(probs * prob_grad, axis=-1, keepdims=True)
        score_grad = (probs * (prob_grad - inner)).astype(bf16)
        qkv_o[0, :, head * HD:(head + 1) * HD] = (dot(score_grad, kh) * root).astype(bf16)
        qkv_o[0, :, width + head * HD:width + (head + 1) * HD] = (
            dot_lt(score_grad, qh) * root
        ).astype(bf16)
        qkv_o[0, :, 2 * width + head * HD:2 * width + (head + 1) * HD] = dot_lt(
            probs.astype(bf16), ah
        ).astype(bf16)
    qg, kg, vg = (qkv_o[0, :, i * width:(i + 1) * width] for i in range(3))
    vec_o[7:8, 0:width] += col_sum(qg.astype(f32))
    vec_o[7:8, width:2 * width] += col_sum(vg.astype(f32))
    for out, at in ((send_o, other), (keep_o, mine)):
        out[0] = dot_rt(qg, wq[at, :]) + dot_rt(kg, wk[at, :]) + dot_rt(vg, wv[at, :])
    full_s[:, mine] = keep_o[0]
    full_s[:, other] = send_o[0]
    grad = full_s[...]
    normed, inv_std = normalize(start)
    vec_o[4:5, :] += col_sum(grad * normed)
    vec_o[5:6, :] += col_sum(grad)
    through = 0.25 * mid_grad_o[0] + norm_back(grad, g1[...].astype(f32), normed, inv_std)
    vec_o[6:7, :] += col_sum(through * m)


def token_kernel(pos, gm, go, mid_grad, tok, mask, token_row, g1, out, full_s):
    half = gm.shape[2]
    full_s[:, pl.ds(pl.multiple_of(pos[4] * half, half), half)] = gm[0]
    full_s[:, pl.ds(pl.multiple_of(pos[5] * half, half), half)] = go[0]
    m = mask[0]
    normed, inv_std = normalize(start_of(tok[0], m, token_row))
    grad = mid_grad[0] + norm_back(full_s[...], g1[...].astype(f32), normed, inv_std)
    out[0] = (grad * (1.0 - m)).astype(bf16)


def out_kernel(pos, gm, go, ab, tok, mask, token_row, s1, db, s2, out, full_s):
    half = gm.shape[2]
    full_s[:, pl.ds(pl.multiple_of(pos[4] * half, half), half)] = gm[0]
    full_s[:, pl.ds(pl.multiple_of(pos[5] * half, half), half)] = go[0]
    mid = start_of(tok[0], mask[0], token_row) + s1[...].astype(f32) * ab[0]
    branch = full_s[...] + db[...].astype(f32)
    out[0] = (mid + s2[...].astype(f32) * branch).astype(bf16)


def whole(array, buffers=None):
    shape = array.shape
    return pl.BlockSpec(shape, lambda *_: (0,) * len(shape))


def per_image(array):
    return pl.BlockSpec((1,) + array.shape[1:], lambda i, *_: (i, 0, 0))


def column_block(rows, width):
    return pl.BlockSpec((rows, width), lambda i, *_: (0, i))


def shaped(*shape, dtype=f32):
    return jax.ShapeDtypeStruct(shape, dtype)


def call(kernel, name, grid, scalars, ins, in_specs, outs, out_specs, scratch=()):
    return pl.pallas_call(
        kernel,
        name=name,
        out_shape=outs,
        grid_spec=pltpu.PrefetchScalarGridSpec(
            num_scalar_prefetch=len(scalars),
            grid=grid,
            in_specs=in_specs,
            out_specs=out_specs,
            scratch_shapes=list(scratch),
        ),
        compiler_params=pltpu.CompilerParams(
            dimension_semantics=("arbitrary",) * len(grid), vmem_limit_bytes=VMEM_LIMIT
        ),
    )(*scalars, *ins)


def per_device(
    tokens, masked_patches, mask_token, norm1_gain, norm1_bias, query_weight, query_bias,
    key_weight, value_weight, value_bias, out_weight, out_bias, attn_scale, norm2_gain,
    norm2_bias, up_weight, up_bias, down_weight, down_bias, mlp_scale, out_cotangent, *, dp, mp,
):
    assert mp == 4 and dp & (dp - 1) == 0
    images, slots = masked_patches.shape
    row_count, model = tokens.shape
    seq_len = row_count // images
    padded = -(-seq_len // 40) * 40
    width = query_weight.shape[1]
    hidden_width = up_weight.shape[1]
    half = model // 2
    chunks = CHUNKS
    count = images // chunks
    rows = count * padded

    m = lax.axis_index("mp")
    core = m & 1
    d = lax.axis_index("dp")
    pos = jnp.stack([m, m ^ 1, m ^ 2, m ^ 3, core, 1 - core]).astype(jnp.int32)

    def to_core(array):
        return lax.ppermute(array, "mp", [(i, i ^ 1) for i in range(mp)])

    def to_x(array):
        return lax.ppermute(array, "mp", [(i, i ^ 2) for i in range(mp)])

    def to_dp(array, bit):
        return lax.ppermute(array, "dp", [(i, i ^ (1 << bit)) for i in range(dp)])

    def sum_mp(send, keep):
        mine = keep + to_core(send)
        mine = mine + to_x(mine)
        return mine, to_core(mine)

    def scatter_dp(array):
        n = dp
        rest = array.shape[1:]
        parts = array.reshape((dp, array.shape[0] // dp) + rest)
        for bit in range(dp.bit_length() - 1):
            n //= 2
            b = (d >> bit) & 1
            parts = parts.reshape((n, 2) + parts.shape[1:])
            send = lax.dynamic_index_in_dim(parts, 1 - b, 1, keepdims=False)
            keep = lax.dynamic_index_in_dim(parts, b, 1, keepdims=False)
            parts = keep + to_dp(send, bit)
        return parts[0]

    row = lambda vector: vector.reshape(1, -1)
    token_row, g1, b1 = row(mask_token), row(norm1_gain), row(norm1_bias)
    g2, b2, s1, s2 = row(norm2_gain), row(norm2_bias), row(attn_scale), row(mlp_scale)
    ob, db, ub = row(out_bias), row(down_bias), row(up_bias)
    bq, bv = row(query_bias), row(value_bias)

    wide = call(
        widen_kernel, "widen", (1,), (), (out_weight,), [whole(out_weight)],
        shaped(width, model), whole(out_weight),
    )
    y = d & 1
    ahead = to_x(lax.dynamic_slice_in_dim(wide, y * (width // 2), width // 2, 0))
    beside = to_dp(ahead, 0)
    from_x = jnp.where(
        y == 0, jnp.concatenate([ahead, beside], 0), jnp.concatenate([beside, ahead], 0)
    )
    from_core, from_far = to_core(wide), to_core(from_x)
    w_parts = (wide, from_core, from_x, from_far)

    def pad(array):
        array = array.reshape(images, seq_len, model)
        return jnp.pad(array, ((0, 0), (0, padded - seq_len), (0, 0)))

    tok_all, cot_all = pad(tokens), pad(out_cotangent)
    patches_all = masked_patches.reshape(images, 1, slots)
    state = []
    for n in range(chunks):
        tok = tok_all[n * count:(n + 1) * count]
        cot = cot_all[n * count:(n + 1) * count]
        patches = patches_all[n * count:(n + 1) * count]
        ins = (tok, patches, token_row, g1, b1, query_weight, bq, key_weight, value_weight, bv)
        outs = (
            shaped(count, padded, 1),
            shaped(count, padded, model, dtype=bf16),
            shaped(count, padded, width, dtype=bf16),
            shaped(count, padded, width, dtype=bf16),
            shaped(count, padded, width, dtype=bf16),
            shaped(count, padded, width),
        )
        mask, attn_in, q, k, v, att = call(
            functools.partial(attend_kernel, seq_len), "attend", (count,), (), ins,
            [per_image(tok), per_image(patches)] + [whole(a) for a in ins[2:]],
            outs, [per_image(a) for a in outs],
        )
        flat = att.reshape(rows, width)
        a_core, a_x = to_core(flat), to_x(flat)
        a_far = to_core(a_x)
        state.append(dict(
            tok=tok, cot=cot, mask=mask, attn_in=attn_in, q=q, k=k, v=v, att=flat,
            a_parts=(flat, a_core, a_x, a_far),
        ))

    blocks = 4
    wide_block = hidden_width // blocks
    for s in state:
        flat2 = lambda a: a.reshape(rows, -1)
        ins = s["a_parts"] + w_parts + (
            ob, s1, g2, b2, flat2(s["tok"]), flat2(s["mask"]), token_row, flat2(s["cot"]), s2,
            up_weight, ub, down_weight,
        )
        specs = [whole(a) for a in ins[:-3]] + [
            column_block(model, wide_block),
            column_block(1, wide_block),
            pl.BlockSpec((wide_block, model), lambda i, *_: (i, 0)),
        ]
        outs = (
            shaped(rows, model), shaped(rows, model, dtype=bf16),
            shaped(rows, hidden_width, dtype=bf16), shaped(rows, hidden_width, dtype=bf16),
            shaped(rows, half), shaped(rows, half), shaped(1, hidden_width), shaped(1, model),
        )
        out_specs = [
            whole(outs[0]), whole(outs[1]), column_block(rows, wide_block),
            column_block(rows, wide_block), whole(outs[4]), whole(outs[5]),
            column_block(1, wide_block), whole(outs[7]),
        ]
        ab, mlp_in, act, hg, send, keep, ubg, dbg = call(
            mlp_kernel, "mlp", (blocks,), (pos,), ins, specs, outs, out_specs,
            (
                pltpu.VMEM((rows, model), bf16), pltpu.VMEM((model, model), bf16),
                pltpu.VMEM((rows, model), bf16),
            ),
        )
        s.update(ab=ab, mlp_in=mlp_in, act=act, hg=hg, ubg=ubg, dbg=dbg)
        s["mlp_in_grad"] = sum_mp(send, keep)

    for s in state:
        ins = (s["act"], down_weight, s["cot"].reshape(rows, model), db)
        outs = (shaped(rows, half), shaped(rows, half), shaped(1, model))
        send, keep, s["scale"] = call(
            down_kernel, "down", (1,), (pos,), ins, [whole(a) for a in ins], outs,
            [whole(a) for a in outs],
        )
        s["mlp_sum"] = sum_mp(send, keep)

    up_grad = scatter_dp(sum(dot_lt(s["mlp_in"], s["hg"]) for s in state))
    out_grads = [
        (s["cot"].reshape(rows, model).astype(f32) * s2.astype(f32)).astype(bf16) for s in state
    ]
    down_grad = scatter_dp(sum(dot_lt(s["act"], g) for s, g in zip(state, out_grads)))

    images3 = lambda a: a.reshape(count, padded, a.shape[-1])
    for s in state:
        gm, go = (images3(a) for a in s["mlp_in_grad"])
        ins = (
            gm, go, s["tok"], s["mask"], images3(s["ab"]), s["cot"], s["q"], s["k"], s["v"],
            token_row, s1, g1, g2, out_weight, query_weight, key_weight, value_weight,
        )
        outs = (
            shaped(count, padded, model), shaped(count, padded, model, dtype=bf16),
            shaped(count, padded, 3 * width, dtype=bf16),
            shaped(count, padded, half), shaped(count, padded, half), shaped(8, model),
        )
        s["mid_grad"], s["attn_grad"], s["qkv_grad"], send, keep, s["vec"] = call(
            functools.partial(back_kernel, seq_len), "back", (count,), (pos,), ins,
            [per_image(a) for a in ins[:9]] + [whole(a) for a in ins[9:]],
            outs, [per_image(a) for a in outs[:5]] + [whole(outs[5])],
            (pltpu.VMEM((padded, model), f32), pltpu.VMEM((padded, width), bf16)),
        )
        s["attn_in_grad"] = sum_mp(send, keep)

    flat2 = lambda a: a.reshape(rows, a.shape[-1])
    out_w_grad = scatter_dp(
        sum(dot_lt(s["att"].astype(bf16), flat2(s["attn_grad"])) for s in state)
    )
    qkv_w_grad = scatter_dp(
        sum(dot_lt(flat2(s["attn_in"]), flat2(s["qkv_grad"])) for s in state)
    )

    vec = sum(s["vec"] for s in state)
    model_rows = jnp.concatenate(
        [
            vec[0:7],
            0.25 * sum(s["dbg"] for s in state),
            sum(s["scale"] for s in state),
        ],
        0,
    )
    model_rows = model_rows + to_core(model_rows)
    model_rows = model_rows + to_x(model_rows)
    per_dp = lambda a: a.reshape(a.shape[0], dp, -1).transpose(1, 0, 2).reshape(dp, -1)
    small = jnp.concatenate(
        [
            per_dp(model_rows), per_dp(vec[7:8, 0:width]), per_dp(vec[7:8, width:2 * width]),
            per_dp(sum(s["ubg"] for s in state)),
        ],
        1,
    )
    small = scatter_dp(small).reshape(-1)
    piece, thin = model // dp, width // dp
    parts = [small[i * piece:(i + 1) * piece] for i in range(9)]
    gain_two, bias_two, scale_one, out_b, gain_one, bias_one, mask_row, down_b, scale_two = parts
    at = 9 * piece
    query_b, value_b = small[at:at + thin], small[at + thin:at + 2 * thin]
    up_b = small[at + 2 * thin:]

    out_rows, token_rows = [], []
    for s in state:
        gm, go = (images3(a) for a in s["attn_in_grad"])
        ins = (gm, go, s["mid_grad"], s["tok"], s["mask"], token_row, g1)
        out = shaped(count, padded, model, dtype=bf16)
        token_rows.append(call(
            token_kernel, "token", (count,), (pos,), ins,
            [per_image(a) for a in ins[:5]] + [whole(a) for a in ins[5:]],
            out, per_image(out), (pltpu.VMEM((padded, model), f32),),
        ))
        gm, go = (images3(a) for a in s["mlp_sum"])
        ins = (gm, go, images3(s["ab"]), s["tok"], s["mask"], token_row, s1, db, s2)
        out_rows.append(call(
            out_kernel, "block_out", (count,), (pos,), ins,
            [per_image(a) for a in ins[:5]] + [whole(a) for a in ins[5:]],
            out, per_image(out), (pltpu.VMEM((padded, model), f32),),
        ))

    def unpad(parts):
        return jnp.concatenate(
            [a[:, :seq_len].reshape(count * seq_len, model) for a in parts], 0
        )

    return (
        unpad(out_rows), unpad(token_rows), mask_row, gain_one, bias_one,
        qkv_w_grad[:, :width], query_b, qkv_w_grad[:, width:2 * width],
        qkv_w_grad[:, 2 * width:], value_b, out_w_grad, out_b, scale_one, gain_two, bias_two,
        up_grad, up_b, down_grad, down_b, scale_two,
    )


def solution(mesh):
    placed = (
        P("dp", None), P("dp", None), P(), P(), P(), P(None, "mp"), P("mp"), P(None, "mp"),
        P(None, "mp"), P("mp"), P("mp", None), P(), P(), P(), P(), P(None, "mp"), P("mp"),
        P("mp", None), P(), P(), P("dp", None),
    )
    sizes = dict(mesh.shape)
    return jax.shard_map(
        functools.partial(per_device, dp=sizes["dp"], mp=sizes["mp"]),
        mesh=mesh,
        in_specs=placed,
        out_specs=(
            P("dp", None), P("dp", None), P("dp"), P("dp"), P("dp"), P("dp", "mp"),
            P(("mp", "dp")), P("dp", "mp"), P("dp", "mp"), P(("mp", "dp")),
            P(("mp", "dp"), None), P("dp"), P("dp"), P("dp"), P("dp"), P("dp", "mp"),
            P(("mp", "dp")), P(("mp", "dp"), None), P("dp"), P("dp"),
        ),
        check_vma=False,
    )
```

```python
import functools
import math

import jax
import jax.numpy as jnp
from jax import lax
from jax.experimental import pallas as pl
from jax.experimental.pallas import tpu as pltpu
from jax.sharding import PartitionSpec as P


HD = 64
CHUNKS = 2
NORM_EPS = 1e-06
ROOT_HALF = 0.7071067811865476
INV_ROOT_TAU = 0.3989422804014327
VMEM_LIMIT = 60 << 20

f32 = jnp.float32
bf16 = jnp.bfloat16


def dot(left, right):
    return lax.dot_general(left, right, (((1,), (0,)), ((), ())), preferred_element_type=f32)


def dot_lt(left, right):
    return lax.dot_general(left, right, (((0,), (0,)), ((), ())), preferred_element_type=f32)


def dot_rt(left, right):
    return lax.dot_general(left, right, (((1,), (1,)), ((), ())), preferred_element_type=f32)


def normalize(values):
    centered = values - jnp.mean(values, axis=-1, keepdims=True)
    inv_std = lax.rsqrt(jnp.mean(centered * centered, axis=-1, keepdims=True) + NORM_EPS)
    return centered * inv_std, inv_std


def norm_back(grad, gain, normed, inv_std):
    scaled = grad * gain
    return inv_std * (
        scaled
        - jnp.mean(scaled, axis=-1, keepdims=True)
        - normed * jnp.mean(scaled * normed, axis=-1, keepdims=True)
    )


def col_sum(values):
    return jnp.sum(values, axis=0, keepdims=True)


def start_of(tok, mask, token_row):
    return tok.astype(f32) * (1.0 - mask) + mask * token_row[...].astype(f32)


def head_probs(queries, keys, seq_len):
    scores = dot_rt(queries, keys) * (1.0 / math.sqrt(HD))
    valid = lax.broadcasted_iota(jnp.int32, scores.shape, 1) < seq_len
    scores = jnp.where(valid, scores, -1e30)
    top = jnp.max(scores, axis=-1, keepdims=True)
    weights = jnp.exp(scores - top)
    return weights * (1.0 / jnp.sum(weights, axis=-1, keepdims=True))


def attend_kernel(
    seq_len, tok, patches, token_row, gain, bias, wq, bq, wk, wv, bv,
    mask_o, attn_in_o, q_o, k_o, v_o, att_o,
):
    rows = tok.shape[1]
    slots = patches.shape[2]
    place = lax.broadcasted_iota(jnp.int32, (rows, slots), 0)
    named = (jnp.broadcast_to(patches[0], (rows, slots)) == place) & (place >= 1)
    mask = jnp.max(jnp.where(named, 1.0, 0.0), axis=-1, keepdims=True)
    mask_o[0] = mask
    normed, _ = normalize(start_of(tok[0], mask, token_row))
    attn_in = (normed * gain[...].astype(f32) + bias[...].astype(f32)).astype(bf16)
    attn_in_o[0] = attn_in
    q_o[0] = (dot(attn_in, wq[...]) + bq[...].astype(f32)).astype(bf16)
    k_o[0] = dot(attn_in, wk[...]).astype(bf16)
    v_o[0] = (dot(attn_in, wv[...]) + bv[...].astype(f32)).astype(bf16)
    for head in range(wq.shape[1] // HD):
        at = slice(head * HD, (head + 1) * HD)
        probs = head_probs(q_o[0, :, at], k_o[0, :, at], seq_len)
        att_o[0, :, at] = dot(probs.astype(bf16), v_o[0, :, at]).astype(bf16).astype(f32)


def widen_kernel(w, o):
    o[...] = w[...].astype(f32)


def mlp_kernel(
    pos, a0, a1, a2, a3, w0, w1, w2, w3, ob, s1, g2, b2, tok, mask, token_row, cot, s2, up, ub, down,
    ab_o, mlp_in_o, act_o, hg_o, send_o, keep_o, ubg_o, dbg_o, att_s, w_s, og_s,
):
    step = pl.program_id(0)
    rows = mlp_in_o.shape[0]
    width = a0.shape[1]
    half = keep_o.shape[1]

    @pl.when(step == 0)
    def _():
        for k, (a, w) in enumerate(((a0, w0), (a1, w1), (a2, w2), (a3, w3))):
            at = pl.ds(pl.multiple_of(pos[k] * width, width), width)
            att_s[:, at] = a[...].astype(bf16)
            w_s[at, :] = w[...].astype(bf16)
        ab_o[...] = dot(att_s[...], w_s[...]) + ob[...].astype(f32)
        send_o[...] = jnp.zeros_like(send_o)
        keep_o[...] = jnp.zeros_like(keep_o)
        dbg_o[...] = jnp.zeros_like(dbg_o)
        block = 40

        def one(i, carry):
            at = pl.ds(pl.multiple_of(i * block, block), block)
            mid = start_of(tok[at, :], mask[at, :], token_row) + s1[...].astype(f32) * ab_o[at, :]
            normed, _ = normalize(mid)
            mlp_in_o[at, :] = (normed * g2[...].astype(f32) + b2[...].astype(f32)).astype(bf16)
            scaled = cot[at, :].astype(f32) * s2[...].astype(f32)
            og_s[at, :] = scaled.astype(bf16)
            dbg_o[...] += col_sum(scaled)
            return carry

        lax.fori_loop(0, rows // block, one, 0)

    hidden = dot(mlp_in_o[...], up[...]) + ub[...].astype(f32)
    cdf = 0.5 * (1.0 + lax.erf(hidden * ROOT_HALF))
    pdf = jnp.exp(-0.5 * hidden * hidden) * INV_ROOT_TAU
    act_o[...] = (hidden * cdf).astype(bf16)
    act_grad = dot_rt(og_s[...], down[...])
    hg = (act_grad * (cdf + hidden * pdf)).astype(bf16)
    hg_o[...] = hg
    ubg_o[...] = col_sum(hg.astype(f32))
    mine = pl.ds(pl.multiple_of(pos[4] * half, half), half)
    other = pl.ds(pl.multiple_of(pos[5] * half, half), half)
    send_o[...] += dot_rt(hg, up[other, :])
    keep_o[...] += dot_rt(hg, up[mine, :])


def down_kernel(pos, act, down, cot, db, send_o, keep_o, scale_o):
    half = keep_o.shape[1]
    mine = pl.ds(pl.multiple_of(pos[4] * half, half), half)
    other = pl.ds(pl.multiple_of(pos[5] * half, half), half)
    send_o[...] = dot(act[...], down[:, other])
    keep_o[...] = dot(act[...], down[:, mine])
    scale_o[:, other] = col_sum(
        cot[:, other].astype(f32) * (send_o[...] + 0.25 * db[:, other].astype(f32))
    )
    scale_o[:, mine] = col_sum(
        cot[:, mine].astype(f32) * (keep_o[...] + 0.25 * db[:, mine].astype(f32))
    )


def back_kernel(
    seq_len, pos, gm, go, tok, mask, ab, cot, q, k, v, token_row, s1, g1, g2, wo, wq, wk, wv,
    mid_grad_o, attn_grad_o, qkv_o, send_o, keep_o, vec_o, full_s, ag_s,
):
    step = pl.program_id(0)
    half = gm.shape[2]
    width = q.shape[2]
    mine = pl.ds(pl.multiple_of(pos[4] * half, half), half)
    other = pl.ds(pl.multiple_of(pos[5] * half, half), half)

    @pl.when(step == 0)
    def _():
        vec_o[...] = jnp.zeros_like(vec_o)

    full_s[:, mine] = gm[0]
    full_s[:, other] = go[0]
    m = mask[0]
    start = start_of(tok[0], m, token_row)
    scale = s1[...].astype(f32)
    branch = ab[0]
    normed, inv_std = normalize(start + scale * branch)
    grad = full_s[...]
    vec_o[0:1, :] += 0.25 * col_sum(grad * normed)
    vec_o[1:2, :] += 0.25 * col_sum(grad)
    mid_grad = cot[0].astype(f32) + norm_back(grad, g2[...].astype(f32), normed, inv_std)
    mid_grad_o[0] = mid_grad
    vec_o[2:3, :] += 0.25 * col_sum(mid_grad * branch)
    scaled = mid_grad * scale
    vec_o[3:4, :] += 0.25 * col_sum(scaled)
    attn_grad_o[0] = scaled.astype(bf16)
    ag_s[...] = dot_rt(attn_grad_o[0], wo[...]).astype(bf16)
    root = 1.0 / math.sqrt(HD)
    for head in range(width // HD):
        at = slice(head * HD, (head + 1) * HD)
        qh, kh, vh, ah = q[0, :, at], k[0, :, at], v[0, :, at], ag_s[:, at]
        probs = head_probs(qh, kh, seq_len)
        prob_grad = dot_rt(ah, vh)
        inner = jnp.sum(probs * prob_grad, axis=-1, keepdims=True)
        score_grad = (probs * (prob_grad - inner)).astype(bf16)
        qkv_o[0, :, head * HD:(head + 1) * HD] = (dot(score_grad, kh) * root).astype(bf16)
        qkv_o[0, :, width + head * HD:width + (head + 1) * HD] = (
            dot_lt(score_grad, qh) * root
        ).astype(bf16)
        qkv_o[0, :, 2 * width + head * HD:2 * width + (head + 1) * HD] = dot_lt(
            probs.astype(bf16), ah
        ).astype(bf16)
    qg, kg, vg = (qkv_o[0, :, i * width:(i + 1) * width] for i in range(3))
    vec_o[7:8, 0:width] += col_sum(qg.astype(f32))
    vec_o[7:8, width:2 * width] += col_sum(vg.astype(f32))
    for out, at in ((send_o, other), (keep_o, mine)):
        out[0] = dot_rt(qg, wq[at, :]) + dot_rt(kg, wk[at, :]) + dot_rt(vg, wv[at, :])
    full_s[:, mine] = keep_o[0]
    full_s[:, other] = send_o[0]
    grad = full_s[...]
    normed, inv_std = normalize(start)
    vec_o[4:5, :] += col_sum(grad * normed)
    vec_o[5:6, :] += col_sum(grad)
    through = 0.25 * mid_grad_o[0] + norm_back(grad, g1[...].astype(f32), normed, inv_std)
    vec_o[6:7, :] += col_sum(through * m)


def token_kernel(pos, gm, go, mid_grad, tok, mask, token_row, g1, out, full_s):
    half = gm.shape[2]
    full_s[:, pl.ds(pl.multiple_of(pos[4] * half, half), half)] = gm[0]
    full_s[:, pl.ds(pl.multiple_of(pos[5] * half, half), half)] = go[0]
    m = mask[0]
    normed, inv_std = normalize(start_of(tok[0], m, token_row))
    grad = mid_grad[0] + norm_back(full_s[...], g1[...].astype(f32), normed, inv_std)
    out[0] = (grad * (1.0 - m)).astype(bf16)


def out_kernel(pos, gm, go, ab, tok, mask, token_row, s1, db, s2, out, full_s):
    half = gm.shape[2]
    full_s[:, pl.ds(pl.multiple_of(pos[4] * half, half), half)] = gm[0]
    full_s[:, pl.ds(pl.multiple_of(pos[5] * half, half), half)] = go[0]
    mid = start_of(tok[0], mask[0], token_row) + s1[...].astype(f32) * ab[0]
    branch = full_s[...] + db[...].astype(f32)
    out[0] = (mid + s2[...].astype(f32) * branch).astype(bf16)


def whole(array):
    shape = array.shape
    return pl.BlockSpec(shape, lambda *_: (0,) * len(shape))


def per_image(array):
    return pl.BlockSpec((1,) + array.shape[1:], lambda i, *_: (i, 0, 0))


def column_block(rows, width):
    return pl.BlockSpec((rows, width), lambda i, *_: (0, i))


def shaped(*shape, dtype=f32):
    return jax.ShapeDtypeStruct(shape, dtype)


def call(kernel, grid, scalars, ins, in_specs, outs, out_specs, scratch=()):
    return pl.pallas_call(
        kernel,
        out_shape=outs,
        grid_spec=pltpu.PrefetchScalarGridSpec(
            num_scalar_prefetch=len(scalars),
            grid=grid,
            in_specs=in_specs,
            out_specs=out_specs,
            scratch_shapes=list(scratch),
        ),
        compiler_params=pltpu.CompilerParams(
            dimension_semantics=("arbitrary",) * len(grid), vmem_limit_bytes=VMEM_LIMIT
        ),
    )(*scalars, *ins)


def per_device(
    tokens, masked_patches, mask_token, norm1_gain, norm1_bias, query_weight, query_bias,
    key_weight, value_weight, value_bias, out_weight, out_bias, attn_scale, norm2_gain,
    norm2_bias, up_weight, up_bias, down_weight, down_bias, mlp_scale, out_cotangent, *, dp, mp,
):
    assert mp == 4 and dp & (dp - 1) == 0
    images, slots = masked_patches.shape
    row_count, model = tokens.shape
    seq_len = row_count // images
    padded = -(-seq_len // 40) * 40
    width = query_weight.shape[1]
    hidden_width = up_weight.shape[1]
    half = model // 2
    chunks = CHUNKS
    count = images // chunks
    rows = count * padded

    m = lax.axis_index("mp")
    core = m & 1
    d = lax.axis_index("dp")
    pos = jnp.stack([m, m ^ 1, m ^ 2, m ^ 3, core, 1 - core]).astype(jnp.int32)

    def to_core(array):
        return lax.ppermute(array, "mp", [(i, i ^ 1) for i in range(mp)])

    def to_x(array):
        return lax.ppermute(array, "mp", [(i, i ^ 2) for i in range(mp)])

    def to_dp(array, bit):
        return lax.ppermute(array, "dp", [(i, i ^ (1 << bit)) for i in range(dp)])

    def sum_mp(send, keep):
        mine = keep + to_core(send)
        mine = mine + to_x(mine)
        return mine, to_core(mine)

    def scatter_dp(array):
        n = dp
        rest = array.shape[1:]
        parts = array.reshape((dp, array.shape[0] // dp) + rest)
        for bit in range(dp.bit_length() - 1):
            n //= 2
            b = (d >> bit) & 1
            parts = parts.reshape((n, 2) + parts.shape[1:])
            send = lax.dynamic_index_in_dim(parts, 1 - b, 1, keepdims=False)
            keep = lax.dynamic_index_in_dim(parts, b, 1, keepdims=False)
            parts = keep + to_dp(send, bit)
        return parts[0]

    row = lambda vector: vector.reshape(1, -1)
    token_row, g1, b1 = row(mask_token), row(norm1_gain), row(norm1_bias)
    g2, b2, s1, s2 = row(norm2_gain), row(norm2_bias), row(attn_scale), row(mlp_scale)
    ob, db, ub = row(out_bias), row(down_bias), row(up_bias)
    bq, bv = row(query_bias), row(value_bias)

    wide = call(
        widen_kernel, (1,), (), (out_weight,), [whole(out_weight)],
        shaped(width, model), whole(out_weight),
    )
    y = d & 1
    ahead = to_x(lax.dynamic_slice_in_dim(wide, y * (width // 2), width // 2, 0))
    beside = to_dp(ahead, 0)
    from_x = jnp.where(
        y == 0, jnp.concatenate([ahead, beside], 0), jnp.concatenate([beside, ahead], 0)
    )
    from_core = to_core(wide)
    from_far = to_core(from_x)
    w_parts = (wide, from_core, from_x, from_far)

    def pad(array):
        array = array.reshape(images, seq_len, model)
        return jnp.pad(array, ((0, 0), (0, padded - seq_len), (0, 0)))

    tok_all = pad(tokens)
    cot_all = pad(out_cotangent)
    patches_all = masked_patches.reshape(images, 1, slots)
    state = []
    for n in range(chunks):
        tok = tok_all[n * count:(n + 1) * count]
        cot = cot_all[n * count:(n + 1) * count]
        patches = patches_all[n * count:(n + 1) * count]
        ins = (tok, patches, token_row, g1, b1, query_weight, bq, key_weight, value_weight, bv)
        outs = (
            shaped(count, padded, 1),
            shaped(count, padded, model, dtype=bf16),
            shaped(count, padded, width, dtype=bf16),
            shaped(count, padded, width, dtype=bf16),
            shaped(count, padded, width, dtype=bf16),
            shaped(count, padded, width),
        )
        mask, attn_in, q, k, v, att = call(
            functools.partial(attend_kernel, seq_len), (count,), (), ins,
            [per_image(tok), per_image(patches)] + [whole(a) for a in ins[2:]],
            outs, [per_image(a) for a in outs],
        )
        flat = att.reshape(rows, width)
        a_core = to_core(flat)
        a_x = to_x(flat)
        a_far = to_core(a_x)
        state.append(dict(
            tok=tok, cot=cot, mask=mask, attn_in=attn_in, q=q, k=k, v=v, att=flat,
            a_parts=(flat, a_core, a_x, a_far),
        ))

    blocks = 4
    wide_block = hidden_width // blocks
    for s in state:
        flat2 = lambda a: a.reshape(rows, -1)
        ins = s["a_parts"] + w_parts + (
            ob, s1, g2, b2, flat2(s["tok"]), flat2(s["mask"]), token_row, flat2(s["cot"]), s2,
            up_weight, ub, down_weight,
        )
        specs = [whole(a) for a in ins[:-3]] + [
            column_block(model, wide_block),
            column_block(1, wide_block),
            pl.BlockSpec((wide_block, model), lambda i, *_: (i, 0)),
        ]
        outs = (
            shaped(rows, model), shaped(rows, model, dtype=bf16),
            shaped(rows, hidden_width, dtype=bf16), shaped(rows, hidden_width, dtype=bf16),
            shaped(rows, half), shaped(rows, half), shaped(1, hidden_width), shaped(1, model),
        )
        out_specs = [
            whole(outs[0]), whole(outs[1]), column_block(rows, wide_block),
            column_block(rows, wide_block), whole(outs[4]), whole(outs[5]),
            column_block(1, wide_block), whole(outs[7]),
        ]
        ab, mlp_in, act, hg, send, keep, ubg, dbg = call(
            mlp_kernel, (blocks,), (pos,), ins, specs, outs, out_specs,
            (
                pltpu.VMEM((rows, model), bf16), pltpu.VMEM((model, model), bf16),
                pltpu.VMEM((rows, model), bf16),
            ),
        )
        s.update(ab=ab, mlp_in=mlp_in, act=act, hg=hg, ubg=ubg, dbg=dbg)
        s["mlp_in_grad"] = sum_mp(send, keep)

    for s in state:
        ins = (s["act"], down_weight, s["cot"].reshape(rows, model), db)
        outs = (shaped(rows, half), shaped(rows, half), shaped(1, model))
        send, keep, s["scale"] = call(
            down_kernel, (1,), (pos,), ins, [whole(a) for a in ins], outs,
            [whole(a) for a in outs],
        )
        s["mlp_sum"] = sum_mp(send, keep)

    up_grad = sum(dot_lt(s["mlp_in"], s["hg"]) for s in state)
    up_grad = scatter_dp(up_grad)
    out_grads = [
        (s["cot"].reshape(rows, model).astype(f32) * s2.astype(f32)).astype(bf16) for s in state
    ]
    down_grad = sum(dot_lt(s["act"], g) for s, g in zip(state, out_grads))
    down_grad = scatter_dp(down_grad)

    images3 = lambda a: a.reshape(count, padded, a.shape[-1])
    for s in state:
        gm, go = (images3(a) for a in s["mlp_in_grad"])
        ins = (
            gm, go, s["tok"], s["mask"], images3(s["ab"]), s["cot"], s["q"], s["k"], s["v"],
            token_row, s1, g1, g2, out_weight, query_weight, key_weight, value_weight,
        )
        outs = (
            shaped(count, padded, model), shaped(count, padded, model, dtype=bf16),
            shaped(count, padded, 3 * width, dtype=bf16),
            shaped(count, padded, half), shaped(count, padded, half), shaped(8, model),
        )
        s["mid_grad"], s["attn_grad"], s["qkv_grad"], send, keep, s["vec"] = call(
            functools.partial(back_kernel, seq_len), (count,), (pos,), ins,
            [per_image(a) for a in ins[:9]] + [whole(a) for a in ins[9:]],
            outs, [per_image(a) for a in outs[:5]] + [whole(outs[5])],
            (pltpu.VMEM((padded, model), f32), pltpu.VMEM((padded, width), bf16)),
        )
        s["attn_in_grad"] = sum_mp(send, keep)

    flat2 = lambda a: a.reshape(rows, a.shape[-1])
    out_w_grad = sum(dot_lt(s["att"].astype(bf16), flat2(s["attn_grad"])) for s in state)
    qkv_w_grad = sum(dot_lt(flat2(s["attn_in"]), flat2(s["qkv_grad"])) for s in state)
    qkv_w_grad = scatter_dp(qkv_w_grad)
    out_w_grad = scatter_dp(out_w_grad)

    vec = sum(s["vec"] for s in state)
    model_rows = jnp.concatenate(
        [
            vec[0:7],
            0.25 * sum(s["dbg"] for s in state),
            sum(s["scale"] for s in state),
        ],
        0,
    )
    model_rows = model_rows + to_core(model_rows)
    model_rows = model_rows + to_x(model_rows)
    per_dp = lambda a: a.reshape(a.shape[0], dp, -1).transpose(1, 0, 2).reshape(dp, -1)
    small = jnp.concatenate(
        [
            per_dp(model_rows), per_dp(vec[7:8, 0:width]), per_dp(vec[7:8, width:2 * width]),
            per_dp(sum(s["ubg"] for s in state)),
        ],
        1,
    )
    small = scatter_dp(small).reshape(-1)
    piece, thin = model // dp, width // dp
    parts = [small[i * piece:(i + 1) * piece] for i in range(9)]
    gain_two, bias_two, scale_one, out_b, gain_one, bias_one, mask_row, down_b, scale_two = parts
    at = 9 * piece
    query_b, value_b = small[at:at + thin], small[at + thin:at + 2 * thin]
    up_b = small[at + 2 * thin:]

    out_rows, token_rows = [], []
    for s in state:
        gm, go = (images3(a) for a in s["attn_in_grad"])
        ins = (gm, go, s["mid_grad"], s["tok"], s["mask"], token_row, g1)
        out = shaped(count, padded, model, dtype=bf16)
        token_rows.append(call(
            token_kernel, (count,), (pos,), ins,
            [per_image(a) for a in ins[:5]] + [whole(a) for a in ins[5:]],
            out, per_image(out), (pltpu.VMEM((padded, model), f32),),
        ))
        gm, go = (images3(a) for a in s["mlp_sum"])
        ins = (gm, go, images3(s["ab"]), s["tok"], s["mask"], token_row, s1, db, s2)
        out_rows.append(call(
            out_kernel, (count,), (pos,), ins,
            [per_image(a) for a in ins[:5]] + [whole(a) for a in ins[5:]],
            out, per_image(out), (pltpu.VMEM((padded, model), f32),),
        ))

    def unpad(parts):
        return jnp.concatenate(
            [a[:, :seq_len].reshape(count * seq_len, model) for a in parts], 0
        )

    return (
        unpad(out_rows), unpad(token_rows), mask_row, gain_one, bias_one,
        qkv_w_grad[:, :width], query_b, qkv_w_grad[:, width:2 * width],
        qkv_w_grad[:, 2 * width:], value_b, out_w_grad, out_b, scale_one, gain_two, bias_two,
        up_grad, up_b, down_grad, down_b, scale_two,
    )


def solution(mesh):
    placed = (
        P("dp", None), P("dp", None), P(), P(), P(), P(None, "mp"), P("mp"), P(None, "mp"),
        P(None, "mp"), P("mp"), P("mp", None), P(), P(), P(), P(), P(None, "mp"), P("mp"),
        P("mp", None), P(), P(), P("dp", None),
    )
    sizes = dict(mesh.shape)

    def step(*arrays):
        return per_device(*arrays, dp=sizes["dp"], mp=sizes["mp"])

    step = jax.shard_map(
        step,
        mesh=mesh,
        in_specs=placed,
        out_specs=(
            P("dp", None), P("dp", None), P("dp"), P("dp"), P("dp"), P("dp", "mp"),
            P(("mp", "dp")), P("dp", "mp"), P("dp", "mp"), P(("mp", "dp")),
            P(("mp", "dp"), None), P("dp"), P("dp"), P("dp"), P("dp"), P("dp", "mp"),
            P(("mp", "dp")), P(("mp", "dp"), None), P("dp"), P("dp"),
        ),
        check_vma=False,
    )
    return step
```
